32 devices in a mesh: seq: 8 (over z, x), var: 4 (over y, core).
Axes of the slice: x: 2, y: 2, z: 4, core: 2. Of those that a mesh axis runs over, the one named last changes fastest.
Arguments:
- clean_proj: bfloat16 [256, 10240], P('seq'), may hold values from -8 to 8
- corrupt_proj: bfloat16 [256, 10240], P('seq'), may hold values from -8 to 8
- patch_pos: int32 [4, 16], P('var'), may hold values from 0 to 255
- patch_mode: int32 [4], P('var'), may hold values from 0 to 2
- a_log: float32 [16, 5120], replicated, may hold values from -6 to 1.5
- dt_bias: float32 [5120], replicated, may hold values from -6 to -2
- conv_weight: float32 [4, 5120], replicated, may hold values from -3 to 3
- conv_bias: float32 [5120], replicated, may hold values from -3 to 3
- x_weight: bfloat16 [5120, 192], replicated, may hold values from -0.078125 to 0.078125
- dt_weight: bfloat16 [160, 5120], replicated, may hold values from -0.5 to 0.5
- d_skip: float32 [5120], replicated, may hold values from 0.5 to 1.5
Outputs:
- patched_out: bfloat16 [4, 256, 5120], P('var', 'seq')
- effect_peak: float32 [4, 5120], P('var')
The draws below stay inside these ranges and needn't reach their ends.
Inputs may be any that keep to these rules, and one draw needn't show every extreme that they name: `patch_pos`: positions of one variant may repeat.
All inputs are finite; a program needn't handle non-finite values.
Results may differ from the reference program's by a relative error of at most 0.0029.
The reference program's roundings to bfloat16 on the way (of `conv_act`, `low_rank` and `patched_in`) count: a program that leaves them out, or rounds other values in their place, can miss the bound.
Values may be sent and summed in bfloat16 or wider, within the bound.
A program may use at most 128 MiB of HBM per device.

```python
import jax
import jax.numpy as jnp
from jax import lax

INNER = 5120
STATE = 16
RANK = 160
CONV = 4
PATCHES = 16
SEQ = 256
VARS = 4


def paired_inputs(key):
    base_key = jax.random.fold_in(key, 101)
    jitter_key = jax.random.fold_in(key, 202)
    shape_full = (SEQ, 2 * INNER)
    base_values = jax.random.normal(base_key, shape_full, jnp.float32)
    jitter = jax.random.normal(jitter_key, shape_full, jnp.float32)
    position = jnp.arange(SEQ, dtype=jnp.float32) / SEQ
    growth = 1.0 + 2.0 * position
    clean_values = jnp.clip(base_values, -8.0, 8.0)
    corrupt_values = jnp.clip(base_values + 0.6 * growth[:, None] * jitter, -8.0, 8.0)
    return (clean_values, corrupt_values)


def draw_clean_proj(key, part):
    return paired_inputs(key)[0].astype(jnp.bfloat16)


def draw_corrupt_proj(key, part):
    return paired_inputs(key)[1].astype(jnp.bfloat16)


def place_ends(drawn, own_key, smallest, top_value):
    longest = drawn.shape.index(max(drawn.shape))
    spots = []
    for shift in (0, 1):
        where = [jax.random.randint(jax.random.fold_in(own_key, axis), (), 0, length) for axis, length in enumerate(drawn.shape)]
        where[longest] = (where[longest] + shift) % drawn.shape[longest]
        spots.append(tuple(where))
    return drawn.at[spots[0]].set(smallest).at[spots[1]].set(top_value)


def bell_draw(key, dims, width, bound, kind=jnp.bfloat16):
    drawn = width * jax.random.normal(key, dims, jnp.float32)
    return jnp.clip(drawn, min=-bound, max=bound).astype(kind)


def setup_inputs(seed: int = 0) -> dict:
    arg_keys = jax.random.split(jax.random.key(seed), 12)
    return {
        "clean_proj": draw_clean_proj(jax.random.fold_in(arg_keys[11], 71), 0),
        "corrupt_proj": draw_corrupt_proj(jax.random.fold_in(arg_keys[11], 71), 0),
        "patch_pos": place_ends(jax.random.randint(arg_keys[2], (VARS, PATCHES), 0, SEQ), jax.random.fold_in(arg_keys[2], 1), 0, SEQ - 1).astype(jnp.int32),
        "patch_mode": place_ends(jax.random.randint(arg_keys[3], (VARS,), 0, 3), jax.random.fold_in(arg_keys[3], 1), 0, 2).astype(jnp.int32),
        "a_log": jnp.clip(jax.random.uniform(arg_keys[4], (STATE, INNER), jnp.float32, -6.0, 1.5), -6.0, 1.5),
        "dt_bias": jnp.clip(jax.random.uniform(arg_keys[5], (INNER,), jnp.float32, -6.0, -2.0), -6.0, -2.0),
        "conv_weight": bell_draw(arg_keys[6], (CONV, INNER), CONV ** -0.5, 3.0, jnp.float32),
        "conv_bias": bell_draw(arg_keys[7], (INNER,), 0.5, 3.0, jnp.float32),
        "x_weight": bell_draw(arg_keys[8], (INNER, RANK + 2 * STATE), INNER ** -0.5, 0.078125),
        "dt_weight": bell_draw(arg_keys[9], (RANK, INNER), RANK ** -0.5, 0.5),
        "d_skip": jnp.clip(1.0 + 0.1 * jax.random.normal(arg_keys[10], (INNER,), jnp.float32), 0.5, 1.5),
    }


def mixer_run(projection, a_log, dt_bias, conv_weight, conv_bias, x_weight, dt_weight, d_skip):
    length = projection.shape[0]
    signal = projection[:, :INNER].astype(jnp.float32)
    gate_rows = projection[:, INNER:].astype(jnp.float32)
    padded = jnp.concatenate([jnp.zeros((CONV - 1, INNER), jnp.float32), signal], axis=0)
    conv_sum = conv_bias[None, :] + conv_weight[0][None, :] * padded[0:length]
    for lag_index in range(1, CONV):
        conv_sum = conv_sum + conv_weight[lag_index][None, :] * padded[lag_index:lag_index + length]
    conv_act = lax.optimization_barrier(jax.nn.silu(conv_sum).astype(jnp.bfloat16))
    projected = jnp.dot(conv_act, x_weight, preferred_element_type=jnp.float32)
    low_rank = projected[:, :RANK].astype(jnp.bfloat16)
    input_map = projected[:, RANK:RANK + STATE]
    output_map = projected[:, RANK + STATE:]
    step_size = jax.nn.softplus(jnp.dot(low_rank, dt_weight, preferred_element_type=jnp.float32) + dt_bias[None, :])
    decay_rates = jnp.exp(a_log)
    signal_f = conv_act.astype(jnp.float32)

    def stepper(carried, inputs):
        step_row, signal_row, input_vec, output_vec = inputs
        carried = jnp.exp(-step_row[None, :] * decay_rates) * carried + (step_row * signal_row)[None, :] * input_vec[:, None]
        return (carried, lax.optimization_barrier(jnp.sum(output_vec[:, None] * carried, axis=0)))
    final_state, readout = lax.scan(stepper, jnp.zeros((STATE, INNER), jnp.float32), (step_size, signal_f, input_map, output_map))
    result_rows = (readout + d_skip[None, :] * signal_f) * jax.nn.silu(gate_rows)
    return result_rows.astype(jnp.bfloat16)

def reference(clean_proj, corrupt_proj, patch_pos, patch_mode, a_log, dt_bias, conv_weight, conv_bias, x_weight, dt_weight, d_skip):
    clean_out = mixer_run(clean_proj, a_log, dt_bias, conv_weight, conv_bias, x_weight, dt_weight, d_skip)
    corrupt_out = mixer_run(corrupt_proj, a_log, dt_bias, conv_weight, conv_bias, x_weight, dt_weight, d_skip)
    clean_out, corrupt_out = lax.optimization_barrier((clean_out, corrupt_out))
    clean_f = clean_out.astype(jnp.float32)
    corrupt_f = corrupt_out.astype(jnp.float32)
    normalizer = lax.optimization_barrier(jnp.sum((clean_f - corrupt_f) ** 2, axis=0))
    spread = jnp.sqrt(normalizer / SEQ + 1e-06)
    positions = jnp.arange(SEQ, dtype=jnp.int32)
    columns = jnp.arange(2 * INNER, dtype=jnp.int32)

    def variant(payload):
        targets, chosen_mode = payload
        hit_rows = jnp.any(positions[:, None] == targets[None, :], axis=1)
        take_signal = (hit_rows & (chosen_mode != 1))[:, None] & (columns < INNER)[None, :]
        take_gate = (hit_rows & (chosen_mode != 0))[:, None] & (columns >= INNER)[None, :]
        patched_in = jnp.where(take_signal | take_gate, clean_proj, corrupt_proj)
        patched = mixer_run(patched_in, a_log, dt_bias, conv_weight, conv_bias, x_weight, dt_weight, d_skip)
        patched = lax.optimization_barrier(patched)
        peak = lax.optimization_barrier(jnp.max(jnp.abs(patched.astype(jnp.float32) - corrupt_f), axis=0)) / spread
        return (patched, peak)
    patched_out, effect_peak = lax.map(variant, (patch_pos, patch_mode))
    return (patched_out, effect_peak)
```

```python
import functools

import jax
import jax.numpy as jnp
from jax import lax
from jax.experimental import pallas as pl
from jax.experimental.pallas import tpu as pltpu
from jax.sharding import PartitionSpec as P

STATE = 16
RANK = 160
PAD = 8
LOG2E = 1.4426950408889634
TINY = 1e-06
MESH = pl.DeviceIdType.MESH


def lanes(width, most):
    best = 128
    for k in range(1, most // 128 + 1):
        if width % (128 * k) == 0:
            best = 128 * k
    return best


def wide(tile, width):
    return jnp.concatenate([tile] * (width // 128), axis=1)


def body(
    ns, nv,
    clean, corrupt, pos, mode, a_log, dtb, cw, cb, xw, dtw, dsk,
    out, eff,
    tails, rims, ext, act16, act, proj, bsp, csp, rate, stp, acc, run, tot, tot_in,
    ends, even_end, carry, carry_out, cut, whole, own_sq, sq_in, own_pk, pk_in, nrm, nrm_in,
    s_rim, r_rim, s_tot, r_tot, s_even, r_even, s_car, r_car, s_cor, r_cor,
    s_sq, r_sq, s_pk, r_pk, s_nrm, r_nrm,
):
    rows = clean.shape[0]
    inner = cw.shape[1]
    taps = cw.shape[0]
    span = inner // nv
    s = lax.axis_index("seq")
    v = lax.axis_index("var")
    even = lax.rem(s, 2) == 0
    odd = lax.rem(s, 2) == 1

    barrier = pltpu.get_barrier_semaphore()

    def greet(d, _):
        pl.semaphore_signal(barrier, inc=1, device_id={"seq": lax.rem(s + d, ns)}, device_id_type=MESH)
        return 0

    lax.fori_loop(1, ns, greet, 0)
    for d in range(1, nv):
        pl.semaphore_signal(barrier, inc=1, device_id={"var": lax.rem(v + d, nv)}, device_id_type=MESH)

    tails[...] = jnp.concatenate(
        [
            clean[rows - 16 :, :inner].astype(jnp.float32)[8:],
            corrupt[rows - 16 :, :inner].astype(jnp.float32)[8:],
        ],
        axis=0,
    ).astype(jnp.bfloat16)
    pl.semaphore_wait(barrier, ns - 1 + nv - 1)

    def remote(src, dst, send, recv, where):
        return pltpu.make_async_remote_copy(
            src_ref=src, dst_ref=dst, send_sem=send, recv_sem=recv,
            device_id=where, device_id_type=MESH,
        )

    rim_copy = remote(tails, rims, s_rim, r_rim, {"seq": lax.rem(s + 1, ns)})

    @pl.when(s < ns - 1)
    def _():
        rim_copy.start()

    rate[...] = jnp.exp(a_log[...]) * (-LOG2E)
    where_rows = s * rows - PAD + lax.broadcasted_iota(jnp.int32, (rows + PAD, pos.shape[1]), 0)
    hits = jnp.max((where_rows == pos[...]).astype(jnp.float32), axis=1, keepdims=True)
    chosen = mode[...]
    take_signal = hits * (chosen != 1).astype(jnp.float32) > 0.5
    take_gate = (hits * (chosen != 0).astype(jnp.float32) > 0.5)[PAD:]

    @pl.when(s == 0)
    def _():
        rims[...] = jnp.zeros_like(rims)

    @pl.when(s > 0)
    def _():
        rim_copy.wait_recv()

    lb = lanes(inner, 256)

    def conv(i, _):
        col = pl.ds(pl.multiple_of(i * lb, lb), lb)
        edge = rims[:, col].astype(jnp.float32)
        ext[0, 0:PAD, :] = edge[0:8]
        ext[1, 0:PAD, :] = edge[8:16]
        ext[0, PAD:, :] = clean[:, col].astype(jnp.float32)
        ext[1, PAD:, :] = corrupt[:, col].astype(jnp.float32)
        ext[2] = jnp.where(take_signal, ext[0], ext[1])
        for r in range(3):
            total = cb[:, col] + cw[0:1, col] * ext[r, PAD - taps + 1 : PAD - taps + 1 + rows, :]
            for k in range(1, taps):
                first = PAD - taps + 1 + k
                total = total + cw[k : k + 1, col] * ext[r, first : first + rows, :]
            rounded = (total / (1.0 + jnp.exp(-total))).astype(jnp.bfloat16)
            act16[r * rows : (r + 1) * rows, col] = rounded
            act[r, :, col] = rounded.astype(jnp.float32)
        return 0

    lax.fori_loop(0, inner // lb, conv, 0)
    width = xw.shape[1]
    proj[...] = jnp.zeros_like(proj)
    proj[:, :width] = jnp.dot(act16[...], xw[...], preferred_element_type=jnp.float32)
    flipped = proj[:, 128:].T
    first = RANK - 128
    for t in range(3 * rows):
        bsp[t] = jnp.broadcast_to(flipped[first : first + STATE, t : t + 1], (STATE, 128))
        csp[t] = jnp.broadcast_to(flipped[first + STATE : first + 2 * STATE, t : t + 1], (STATE, 128))

    chunks = [(0, v * span), (1, v * span)] + [(2, j * span) for j in range(nv)]
    tb = lanes(span, 256)

    for c, (r, off) in enumerate(chunks):
        low = proj[r * rows : (r + 1) * rows, :RANK].astype(jnp.bfloat16)

        def steps_of(i, _, c=c, off=off, low=low):
            here = pl.ds(pl.multiple_of(i * tb, tb), tb)
            col = pl.ds(pl.multiple_of(off + i * tb, tb), tb)
            raw = jnp.dot(low, dtw[:, col], preferred_element_type=jnp.float32) + dtb[:, col]
            step = jnp.maximum(raw, 0.0) + jnp.log1p(jnp.exp(-jnp.abs(raw)))
            stp[c, :, here] = step
            tot[c, :, here] = jnp.sum(step, axis=0, keepdims=True)
            return 0

        lax.fori_loop(0, span // tb, steps_of, 0)

    partner = {"seq": lax.rem(s + 1, ns)}
    tot_copy = remote(tot, tot_in, s_tot, r_tot, partner)

    @pl.when(even)
    def _():
        tot_copy.start()

    even_copies = [remote(ends.at[c], even_end.at[c], s_even.at[c], r_even.at[c], partner) for c in range(len(chunks))]

    for c, (r, off) in enumerate(chunks):

        def scan_of(i, _, c=c, r=r, off=off):
            here = pl.ds(pl.multiple_of(i * tb, tb), tb)
            col = pl.ds(pl.multiple_of(off + i * tb, tb), tb)
            rates = rate[:, col]

            def eight(b, carried):
                state, running = carried
                at = pl.ds(pl.multiple_of(b * 8, 8), 8)
                steps = stp[c, at, here]
                flows = steps * act[r, at, col]
                outs, sums = [], []
                for k in range(8):
                    step = steps[k : k + 1]
                    t = r * rows + b * 8 + k
                    state = jnp.exp2(rates * step) * state + flows[k : k + 1] * wide(bsp[t], tb)
                    running = running + step
                    outs.append(jnp.sum(wide(csp[t], tb) * state, axis=0, keepdims=True))
                    sums.append(running)
                acc[c, at, here] = jnp.concatenate(outs, axis=0)
                run[c, at, here] = jnp.concatenate(sums, axis=0)
                return state, running

            zero = (jnp.zeros((STATE, tb), jnp.float32), jnp.zeros((1, tb), jnp.float32))
            state, _ = lax.fori_loop(0, rows // 8, eight, zero)
            ends[c, :, here] = state
            return 0

        lax.fori_loop(0, span // tb, scan_of, 0)

        @pl.when(even)
        def _(c=c):
            even_copies[c].start()

    @pl.when(odd)
    def _():
        tot_copy.wait_recv()

    onward = []
    for c in range(len(chunks)):
        onward.append(
            [
                remote(carry_out.at[c], carry.at[c], s_car.at[c, m], r_car.at[c], {"seq": lax.rem(s + 1 + m, ns)})
                for m in range(2)
            ]
        )

    cor_copies = [
        remote(cut.at[1], whole.at[d - 1], s_cor.at[d - 1], r_cor.at[d - 1], {"var": lax.rem(v + d, nv)})
        for d in range(1, nv)
    ]

    def seq_copy(d, src, dst, send, recv):
        return remote(src, dst.at[d - 1], send.at[d - 1], recv.at[d - 1], {"seq": lax.rem(s + d, ns)})

    def start_all(src, dst, send, recv):
        def go(d, _):
            seq_copy(d, src, dst, send, recv).start()
            return 0

        lax.fori_loop(1, ns, go, 0)

    def wait_all(src, dst, send, recv):
        def go(d, _):
            seq_copy(d, src, dst, send, recv).wait()
            return 0

        lax.fori_loop(1, ns, go, 0)

    for c, (r, off) in enumerate(chunks):

        @pl.when(s < 2)
        def _(c=c):
            carry[c] = jnp.zeros((STATE, span), jnp.float32)

        @pl.when(s >= 2)
        def _(c=c):
            onward[c][0].wait_recv()

        @pl.when(odd)
        def _(c=c, off=off):
            even_copies[c].wait_recv()

            def link(i, _):
                here = pl.ds(pl.multiple_of(i * tb, tb), tb)
                col = pl.ds(pl.multiple_of(off + i * tb, tb), tb)
                rates = rate[:, col]
                entering = carry[c, :, here]
                mine = jnp.exp2(rates * tot_in[c, :, here]) * entering + even_end[c, :, here]
                carry_out[c, :, here] = jnp.exp2(rates * tot[c, :, here]) * mine + ends[c, :, here]
                carry[c, :, here] = mine
                return 0

            lax.fori_loop(0, span // tb, link, 0)

        @pl.when(odd & (s < ns - 1))
        def _(c=c):
            onward[c][1].start()
            onward[c][0].start()

    def finish(c, r, off):
        def piece(i, _):
            here = pl.ds(pl.multiple_of(i * tb, tb), tb)
            col = pl.ds(pl.multiple_of(off + i * tb, tb), tb)
            gcol = pl.ds(pl.multiple_of(inner + off + i * tb, tb), tb)
            rates = rate[:, col]
            entering = carry[c, :, here]

            def eight(b, _):
                at = pl.ds(pl.multiple_of(b * 8, 8), 8)
                running = run[c, at, here]
                outs = []
                for k in range(8):
                    t = r * rows + b * 8 + k
                    outs.append(
                        jnp.sum(
                            jnp.exp2(rates * running[k : k + 1]) * (wide(csp[t], tb) * entering),
                            axis=0,
                            keepdims=True,
                        )
                    )
                acc[c, at, here] = acc[c, at, here] + jnp.concatenate(outs, axis=0)
                return 0

            lax.fori_loop(0, rows // 8, eight, 0)
            if r == 0:
                gate = clean[:, gcol].astype(jnp.float32)
            elif r == 1:
                gate = corrupt[:, gcol].astype(jnp.float32)
            else:
                gate = jnp.where(
                    take_gate, clean[:, gcol].astype(jnp.float32), corrupt[:, gcol].astype(jnp.float32)
                )
            silu = gate / (1.0 + jnp.exp(-gate))
            result = ((acc[c, :, here] + dsk[:, col] * act[r, :, col]) * silu).astype(jnp.bfloat16)
            if r < 2:
                cut[r, :, here] = result
            else:
                out[:, col] = result
            return 0

        lax.fori_loop(0, span // tb, piece, 0)

    finish(0, 0, v * span)
    finish(1, 1, v * span)
    for copy in cor_copies:
        copy.start()
    gap = cut[0].astype(jnp.float32) - cut[1].astype(jnp.float32)
    own_sq[...] = jnp.sum(gap * gap, axis=0, keepdims=True)
    start_all(own_sq, sq_in, s_sq, r_sq)
    for c in range(2, len(chunks)):
        finish(c, *chunks[c])
    for copy in cor_copies:
        copy.wait()

    def peak_at(theirs, place):
        col = pl.ds(pl.multiple_of(place * span, 128), span)
        own_pk[:, col] = jnp.max(
            jnp.abs(out[:, col].astype(jnp.float32) - theirs.astype(jnp.float32)), axis=0, keepdims=True
        )

    peak_at(cut[1], v)
    for d in range(1, nv):
        peak_at(whole[d - 1], lax.rem(v + nv - d, nv))
    start_all(own_pk, pk_in, s_pk, r_pk)
    wait_all(own_sq, sq_in, s_sq, r_sq)
    nrm[...] = own_sq[...] + jnp.sum(sq_in[...], axis=0)
    nrm_copies = [
        remote(nrm, nrm_in.at[d - 1], s_nrm.at[d - 1], r_nrm.at[d - 1], {"var": lax.rem(v + d, nv)})
        for d in range(1, nv)
    ]
    for copy in nrm_copies:
        copy.start()
    wait_all(own_pk, pk_in, s_pk, r_pk)
    best = jnp.maximum(own_pk[...], jnp.max(pk_in[...], axis=0))
    own_pk[...] = best
    for copy in nrm_copies:
        copy.wait()

    def settle(squares, place):
        col = pl.ds(pl.multiple_of(place * span, 128), span)
        eff[:, col] = own_pk[:, col] / jnp.sqrt(squares / (rows * ns) + TINY)

    settle(nrm[...], v)
    for d in range(1, nv):
        settle(nrm_in[d - 1], lax.rem(v + nv - d, nv))

    @pl.when(s < ns - 1)
    def _():
        rim_copy.wait_send()

    @pl.when(even)
    def _():
        tot_copy.wait_send()
        for copy in even_copies:
            copy.wait_send()

    @pl.when(odd & (s < ns - 1))
    def _():
        for pair in onward:
            pair[0].wait_send()
            pair[1].wait_send()


def shards(clean, corrupt, pos, mode, a_log, dtb, cw, cb, xw, dtw, dsk):
    ns, nv = lax.axis_size("seq"), lax.axis_size("var")
    rows = clean.shape[0]
    inner = cw.shape[1]
    span = inner // nv
    n = 2 + nv
    f32, b16 = jnp.float32, jnp.bfloat16
    vm = pltpu.VMEM
    dma = pltpu.SemaphoreType.DMA
    lb = lanes(inner, 256)
    out, eff = pl.pallas_call(
        functools.partial(body, ns, nv),
        out_shape=(
            jax.ShapeDtypeStruct((rows, inner), b16),
            jax.ShapeDtypeStruct((1, inner), f32),
        ),
        in_specs=[pl.BlockSpec(memory_space=vm)] * 11,
        out_specs=[pl.BlockSpec(memory_space=vm)] * 2,
        scratch_shapes=[
            vm((16, inner), b16), vm((16, inner), b16),
            vm((3, rows + PAD, lb), f32),
            vm((3 * rows, inner), b16), vm((3, rows, inner), f32),
            vm((3 * rows, 256), f32),
            vm((3 * rows, STATE, 128), f32), vm((3 * rows, STATE, 128), f32),
            vm((STATE, inner), f32),
            vm((n, rows, span), f32), vm((n, rows, span), f32), vm((n, rows, span), f32),
            vm((n, 1, span), f32), vm((n, 1, span), f32),
            vm((n, STATE, span), f32), vm((n, STATE, span), f32),
            vm((n, STATE, span), f32), vm((n, STATE, span), f32),
            vm((2, rows, span), b16), vm((nv - 1, rows, span), b16),
            vm((1, span), f32), vm((ns - 1, 1, span), f32),
            vm((1, inner), f32), vm((ns - 1, 1, inner), f32),
            vm((1, span), f32), vm((nv - 1, 1, span), f32),
            dma, dma, dma, dma,
            dma((n,)), dma((n,)), dma((n, 2)), dma((n,)),
            dma((nv - 1,)), dma((nv - 1,)),
            dma((ns - 1,)), dma((ns - 1,)), dma((ns - 1,)), dma((ns - 1,)),
            dma((nv - 1,)), dma((nv - 1,)),
        ],
        compiler_params=pltpu.CompilerParams(
            collective_id=0, has_side_effects=True, vmem_limit_bytes=60 * 1024 * 1024
        ),
    )(
        clean, corrupt, pos, mode.reshape(1, 1), a_log, dtb.reshape(1, -1), cw,
        cb.reshape(1, -1), xw, dtw, dsk.reshape(1, -1),
    )
    return (out[None], eff)


def solution(mesh):
    return jax.shard_map(
        shards,
        mesh=mesh,
        in_specs=(
            P("seq", None), P("seq", None), P("var", None), P("var"),
            P(), P(), P(), P(), P(), P(), P(),
        ),
        out_specs=(P("var", "seq", None), P("var", None)),
        check_vma=False,
    )
```

```python
import functools

import jax
import jax.numpy as jnp
from jax import lax
from jax.experimental import pallas as pl
from jax.experimental.pallas import tpu as pltpu
from jax.sharding import PartitionSpec as P

STATE = 16
RANK = 160
PAD = 8
LOG2E = 1.4426950408889634
TINY = 1e-06
MESH = pl.DeviceIdType.MESH


def lanes(width, most):
    best = 128
    for k in range(1, most // 128 + 1):
        if width % (128 * k) == 0:
            best = 128 * k
    return best


def wide(tile, width):
    return jnp.concatenate([tile] * (width // 128), axis=1)


def body(
    ns, nv,
    clean, corrupt, pos, mode, a_log, dtb, cw, cb, xw, dtw, dsk,
    out, eff,
    tails, rims, ext, act16, act, proj, bsp, csp, rate, stp, acc, run, tot, tot_in,
    ends, even_end, carry, carry_out, inflow, cut, whole, own_sq, sq_in, own_pk, pk_in, nrm, nrm_all,
    s_rim, r_rim, s_tot, r_tot, s_even, r_even, s_car, s_back, r_car, s_cor, r_cor,
    s_sq, r_sq, s_pk, r_pk, s_nrm, r_nrm,
):
    rows = clean.shape[0]
    inner = cw.shape[1]
    taps = cw.shape[0]
    span = inner // nv
    s = lax.axis_index("seq")
    v = lax.axis_index("var")
    even = lax.rem(s, 2) == 0
    odd = lax.rem(s, 2) == 1

    barrier = pltpu.get_barrier_semaphore()

    def greet(d, _):
        pl.semaphore_signal(barrier, inc=1, device_id={"seq": lax.rem(s + d, ns)}, device_id_type=MESH)
        return 0

    lax.fori_loop(1, ns, greet, 0)
    for d in range(1, nv):
        pl.semaphore_signal(barrier, inc=1, device_id={"var": lax.rem(v + d, nv)}, device_id_type=MESH)

    row_of = lax.broadcasted_iota(jnp.int32, (8, inner), 0)
    tails[...] = jnp.where(
        row_of > 4,
        clean[rows - 16 :, :inner].astype(jnp.float32)[8:],
        pltpu.roll(corrupt[rows - 16 :, :inner].astype(jnp.float32)[8:], 4, 0),
    ).astype(jnp.bfloat16)
    pl.semaphore_wait(barrier, ns - 1 + nv - 1)

    def remote(src, dst, send, recv, where):
        return pltpu.make_async_remote_copy(
            src_ref=src, dst_ref=dst, send_sem=send, recv_sem=recv,
            device_id=where, device_id_type=MESH,
        )

    rim_copy = remote(tails, rims, s_rim, r_rim, {"seq": lax.rem(s + 1, ns)})

    @pl.when(s < ns - 1)
    def _():
        rim_copy.start()

    rate[...] = jnp.exp(a_log[...]) * (-LOG2E)
    where_rows = s * rows - PAD + lax.broadcasted_iota(jnp.int32, (rows + PAD, pos.shape[1]), 0)
    hits = jnp.max((where_rows == pos[...]).astype(jnp.float32), axis=1, keepdims=True)
    chosen = mode[...]
    take_signal = hits * (chosen != 1).astype(jnp.float32) > 0.5
    take_gate = (hits * (chosen != 0).astype(jnp.float32) > 0.5)[PAD:]

    @pl.when(s == 0)
    def _():
        rims[...] = jnp.zeros_like(rims)

    @pl.when(s > 0)
    def _():
        rim_copy.wait_recv()

    lb = lanes(inner, 256)

    def conv(i, _):
        col = pl.ds(pl.multiple_of(i * lb, lb), lb)
        edge = rims[:, col].astype(jnp.float32)
        ext[0, 0:PAD, :] = edge
        ext[1, 0:PAD, :] = pltpu.roll(edge, 4, 0)
        ext[0, PAD:, :] = clean[:, col].astype(jnp.float32)
        ext[1, PAD:, :] = corrupt[:, col].astype(jnp.float32)
        ext[2] = jnp.where(take_signal, ext[0], ext[1])
        for r in range(3):
            total = cb[:, col] + cw[0:1, col] * ext[r, PAD - taps + 1 : PAD - taps + 1 + rows, :]
            for k in range(1, taps):
                first = PAD - taps + 1 + k
                total = total + cw[k : k + 1, col] * ext[r, first : first + rows, :]
            rounded = (total / (1.0 + jnp.exp(-total))).astype(jnp.bfloat16)
            act16[r * rows : (r + 1) * rows, col] = rounded
            act[r, :, col] = rounded.astype(jnp.float32)
        return 0

    lax.fori_loop(0, inner // lb, conv, 0)
    width = xw.shape[0]
    proj[...] = jnp.zeros_like(proj)
    proj[:, :width] = lax.dot_general(
        act16[...], xw[...], (((1,), (1,)), ((), ())), preferred_element_type=jnp.float32
    )
    flipped = proj[:, 128:].T
    first = RANK - 128
    for t in range(3 * rows):
        bsp[t] = jnp.broadcast_to(flipped[first : first + STATE, t : t + 1], (STATE, 128))
        csp[t] = jnp.broadcast_to(flipped[first + STATE : first + 2 * STATE, t : t + 1], (STATE, 128))

    chunks = [(0, v * span), (1, v * span)] + [(2, j * span) for j in range(nv)]
    tb = lanes(span, 256)

    partner = {"seq": lax.rem(s + 1, ns)}
    tot_copies = [remote(tot.at[c], tot_in.at[c], s_tot.at[c], r_tot.at[c], partner) for c in range(len(chunks))]
    even_copies = [remote(ends.at[c], even_end.at[c], s_even.at[c], r_even.at[c], partner) for c in range(len(chunks))]

    for c, (r, off) in enumerate(chunks):
        low = proj[r * rows : (r + 1) * rows, :RANK].astype(jnp.bfloat16)

        def steps_of(i, _, c=c, off=off, low=low):
            here = pl.ds(pl.multiple_of(i * tb, tb), tb)
            col = pl.ds(pl.multiple_of(off + i * tb, tb), tb)
            raw = jnp.dot(low, dtw[:, col], preferred_element_type=jnp.float32) + dtb[:, col]
            step = jnp.maximum(raw, 0.0) + jnp.log1p(jnp.exp(-jnp.abs(raw)))
            stp[c, :, here] = step
            tot[c, :, here] = jnp.sum(step, axis=0, keepdims=True)
            return 0

        lax.fori_loop(0, span // tb, steps_of, 0)

        @pl.when(even)
        def _(c=c):
            tot_copies[c].start()

        def scan_of(i, _, c=c, r=r, off=off):
            here = pl.ds(pl.multiple_of(i * tb, tb), tb)
            col = pl.ds(pl.multiple_of(off + i * tb, tb), tb)
            rates = rate[:, col]

            def eight(b, carried):
                state, running = carried
                at = pl.ds(pl.multiple_of(b * 8, 8), 8)
                steps = stp[c, at, here]
                flows = steps * act[r, at, col]
                outs, sums = [], []
                for k in range(8):
                    step = steps[k : k + 1]
                    t = r * rows + b * 8 + k
                    state = jnp.exp2(rates * step) * state + flows[k : k + 1] * wide(bsp[t], tb)
                    running = running + step
                    outs.append(jnp.sum(wide(csp[t], tb) * state, axis=0, keepdims=True))
                    sums.append(running)
                acc[c, at, here] = jnp.concatenate(outs, axis=0)
                run[c, at, here] = jnp.concatenate(sums, axis=0)
                return state, running

            zero = (jnp.zeros((STATE, tb), jnp.float32), jnp.zeros((1, tb), jnp.float32))
            state, _ = lax.fori_loop(0, rows // 8, eight, zero)
            ends[c, :, here] = state
            return 0

        lax.fori_loop(0, span // tb, scan_of, 0)

        @pl.when(even)
        def _(c=c):
            even_copies[c].start()

    onward = [
        remote(carry_out.at[c], carry.at[c], s_car.at[c], r_car.at[c], {"seq": lax.rem(s + 2, ns)})
        for c in range(len(chunks))
    ]
    beside = [
        remote(carry.at[c], carry.at[c], s_back.at[c], r_car.at[c], {"seq": lax.rem(s + ns - 1, ns)})
        for c in range(len(chunks))
    ]

    cor_copies = [
        remote(cut.at[1], whole.at[v], s_cor.at[d - 1], r_cor.at[d - 1], {"var": lax.rem(v + d, nv)})
        for d in range(1, nv)
    ]

    def sq_copy(d):
        return remote(own_sq, sq_in.at[d - 1], s_sq.at[d - 1], r_sq.at[d - 1], {"seq": lax.rem(s + d, ns)})

    def pk_copy(d, j):
        return remote(
            own_pk.at[j], pk_in.at[d - 1, j], s_pk.at[d - 1, j], r_pk.at[d - 1, j], {"seq": lax.rem(s + d, ns)}
        )

    def each(act_on):
        def go(d, _):
            act_on(d)
            return 0

        lax.fori_loop(1, ns, go, 0)

    def enter(c, r, off):
        @pl.when(s < 2)
        def _():
            carry[c] = jnp.zeros((STATE, span), jnp.float32)

        @pl.when(s >= 2)
        def _():
            onward[c].wait_recv()

        @pl.when(odd)
        def _():
            @pl.when(s >= 2)
            def _():
                beside[c].start()

            tot_copies[c].wait_recv()
            even_copies[c].wait_recv()

            def link(i, _):
                here = pl.ds(pl.multiple_of(i * tb, tb), tb)
                col = pl.ds(pl.multiple_of(off + i * tb, tb), tb)
                rates = rate[:, col]
                mine = jnp.exp2(rates * tot_in[c, :, here]) * carry[c, :, here] + even_end[c, :, here]
                carry_out[c, :, here] = jnp.exp2(rates * tot[c, :, here]) * mine + ends[c, :, here]
                inflow[c, :, here] = mine
                return 0

            lax.fori_loop(0, span // tb, link, 0)

            @pl.when(s < ns - 1)
            def _():
                onward[c].start()

        @pl.when(even)
        def _():
            inflow[c] = carry[c]

    def finish(c, r, off):
        def piece(i, _):
            here = pl.ds(pl.multiple_of(i * tb, tb), tb)
            col = pl.ds(pl.multiple_of(off + i * tb, tb), tb)
            gcol = pl.ds(pl.multiple_of(inner + off + i * tb, tb), tb)
            rates = rate[:, col]
            entering = inflow[c, :, here]

            def eight(b, _):
                at = pl.ds(pl.multiple_of(b * 8, 8), 8)
                running = run[c, at, here]
                outs = []
                for k in range(8):
                    t = r * rows + b * 8 + k
                    outs.append(
                        jnp.sum(
                            jnp.exp2(rates * running[k : k + 1]) * (wide(csp[t], tb) * entering),
                            axis=0,
                            keepdims=True,
                        )
                    )
                acc[c, at, here] = acc[c, at, here] + jnp.concatenate(outs, axis=0)
                return 0

            lax.fori_loop(0, rows // 8, eight, 0)
            if r == 0:
                gate = clean[:, gcol].astype(jnp.float32)
            elif r == 1:
                gate = corrupt[:, gcol].astype(jnp.float32)
            else:
                gate = jnp.where(
                    take_gate, clean[:, gcol].astype(jnp.float32), corrupt[:, gcol].astype(jnp.float32)
                )
            silu = gate / (1.0 + jnp.exp(-gate))
            result = ((acc[c, :, here] + dsk[:, col] * act[r, :, col]) * silu).astype(jnp.bfloat16)
            if r < 2:
                cut[r, :, here] = result
            else:
                out[:, col] = result
            return 0

        lax.fori_loop(0, span // tb, piece, 0)

    for c in range(2):
        enter(c, *chunks[c])
        finish(c, *chunks[c])
    for copy in cor_copies:
        copy.start()
    whole[v] = cut[1]
    gap = cut[0].astype(jnp.float32) - cut[1].astype(jnp.float32)
    own_sq[...] = jnp.sum(gap * gap, axis=0, keepdims=True)
    each(lambda d: sq_copy(d).start())
    nrm_copies = [
        remote(nrm, nrm_all.at[v], s_nrm.at[d - 1], r_nrm.at[d - 1], {"var": lax.rem(v + d, nv)})
        for d in range(1, nv)
    ]
    for j in range(nv):
        c = 2 + j
        enter(c, *chunks[c])
        finish(c, *chunks[c])
        if j == 0:
            for copy in cor_copies:
                copy.wait()
        if j == nv - 1:
            each(lambda d: sq_copy(d).wait())
            nrm[...] = own_sq[...] + jnp.sum(sq_in[...], axis=0)
            for copy in nrm_copies:
                copy.start()
            nrm_all[v] = nrm[...]
        mine = out[:, j * span : (j + 1) * span].astype(jnp.float32)
        own_pk[j] = jnp.max(jnp.abs(mine - whole[j].astype(jnp.float32)), axis=0, keepdims=True)
        each(lambda d, j=j: pk_copy(d, j).start())
    for copy in nrm_copies:
        copy.wait()
    for j in range(nv):
        each(lambda d, j=j: pk_copy(d, j).wait())
        best = jnp.maximum(own_pk[j], jnp.max(pk_in[:, j], axis=0))
        eff[:, j * span : (j + 1) * span] = best / jnp.sqrt(nrm_all[j] / (rows * ns) + TINY)

    @pl.when(s < ns - 1)
    def _():
        rim_copy.wait_send()

    @pl.when(even)
    def _():
        for c in range(len(chunks)):
            tot_copies[c].wait_send()
            even_copies[c].wait_send()

    @pl.when(odd & (s >= 2))
    def _():
        for copy in beside:
            copy.wait_send()

    @pl.when(odd & (s < ns - 1))
    def _():
        for copy in onward:
            copy.wait_send()


def shards(clean, corrupt, pos, mode, a_log, dtb, cw, cb, xw, dtw, dsk):
    ns, nv = lax.axis_size("seq"), lax.axis_size("var")
    rows = clean.shape[0]
    inner = cw.shape[1]
    span = inner // nv
    n = 2 + nv
    f32, b16 = jnp.float32, jnp.bfloat16
    vm = pltpu.VMEM
    dma = pltpu.SemaphoreType.DMA
    lb = lanes(inner, 256)
    out, eff = pl.pallas_call(
        functools.partial(body, ns, nv),
        out_shape=(
            jax.ShapeDtypeStruct((rows, inner), b16),
            jax.ShapeDtypeStruct((1, inner), f32),
        ),
        in_specs=[pl.BlockSpec(memory_space=vm)] * 11,
        out_specs=[pl.BlockSpec(memory_space=vm)] * 2,
        scratch_shapes=[
            vm((8, inner), b16), vm((8, inner), b16),
            vm((3, rows + PAD, lb), f32),
            vm((3 * rows, inner), b16), vm((3, rows, inner), f32),
            vm((3 * rows, 256), f32),
            vm((3 * rows, STATE, 128), f32), vm((3 * rows, STATE, 128), f32),
            vm((STATE, inner), f32),
            vm((n, rows, span), f32), vm((n, rows, span), f32), vm((n, rows, span), f32),
            vm((n, 1, span), f32), vm((n, 1, span), f32),
            vm((n, STATE, span), f32), vm((n, STATE, span), f32),
            vm((n, STATE, span), f32), vm((n, STATE, span), f32), vm((n, STATE, span), f32),
            vm((2, rows, span), b16), vm((nv, rows, span), b16),
            vm((1, span), f32), vm((ns - 1, 1, span), f32),
            vm((nv, 1, span), f32), vm((ns - 1, nv, 1, span), f32),
            vm((1, span), f32), vm((nv, 1, span), f32),
            dma, dma, dma((n,)), dma((n,)),
            dma((n,)), dma((n,)), dma((n,)), dma((n,)), dma((n,)),
            dma((nv - 1,)), dma((nv - 1,)),
            dma((ns - 1,)), dma((ns - 1,)), dma((ns - 1, nv)), dma((ns - 1, nv)),
            dma((nv - 1,)), dma((nv - 1,)),
        ],
        compiler_params=pltpu.CompilerParams(
            collective_id=0, has_side_effects=True, vmem_limit_bytes=60 * 1024 * 1024
        ),
    )(
        clean, corrupt, pos, mode.reshape(1, 1), a_log, dtb.reshape(1, -1), cw,
        cb.reshape(1, -1), xw.T, dtw, dsk.reshape(1, -1),
    )
    return (out[None], eff)


def solution(mesh):
    return jax.shard_map(
        shards,
        mesh=mesh,
        in_specs=(
            P("seq", None), P("seq", None), P("var", None), P("var"),
            P(), P(), P(), P(), P(), P(), P(),
        ),
        out_specs=(P("var", "seq", None), P("var", None)),
        check_vma=False,
    )
```

```python
import functools

import jax
import jax.numpy as jnp
from jax import lax
from jax.experimental import pallas as pl
from jax.experimental.pallas import tpu as pltpu
from jax.sharding import PartitionSpec as P

STATE = 16
RANK = 160
PAD = 8
LOG2E = 1.4426950408889634
TINY = 1e-06
MESH = pl.DeviceIdType.MESH


def lanes(width, most):
    best = 128
    for k in range(1, most // 128 + 1):
        if width % (128 * k) == 0:
            best = 128 * k
    return best


def wide(tile, width):
    return jnp.concatenate([tile] * (width // 128), axis=1)


def body(
    ns, nv,
    clean, corrupt, pos, mode, a_log, dtb, cw, cb, xw, dtw, dsk,
    out, eff,
    tails, rims, ext, act16, act, proj, bsp, csp, rate, stp, acc, run, tot, tot_in,
    ends, even_end, carry, carry_out, inflow, cut, whole, own_sq, sq_in, own_pk, pk_in, nrm, nrm_all,
    s_rim, r_rim, s_tot, r_tot, s_even, r_even, s_car, s_back, r_car, s_cor, r_cor,
    s_sq, r_sq, s_pk, r_pk, s_nrm, r_nrm,
):
    rows = clean.shape[0]
    inner = cw.shape[1]
    taps = cw.shape[0]
    span = inner // nv
    s = lax.axis_index("seq")
    v = lax.axis_index("var")
    even = lax.rem(s, 2) == 0
    odd = lax.rem(s, 2) == 1

    barrier = pltpu.get_barrier_semaphore()

    def greet(d, _):
        pl.semaphore_signal(barrier, inc=1, device_id={"seq": lax.rem(s + d, ns)}, device_id_type=MESH)
        return 0

    lax.fori_loop(1, ns, greet, 0)
    for d in range(1, nv):
        pl.semaphore_signal(barrier, inc=1, device_id={"var": lax.rem(v + d, nv)}, device_id_type=MESH)

    row_of = lax.broadcasted_iota(jnp.int32, (8, inner), 0)
    tails[...] = jnp.where(
        row_of > 4,
        clean[rows - 16 :, :inner].astype(jnp.float32)[8:],
        pltpu.roll(corrupt[rows - 16 :, :inner].astype(jnp.float32)[8:], 4, 0),
    ).astype(jnp.bfloat16)
    pl.semaphore_wait(barrier, ns - 1 + nv - 1)

    def remote(src, dst, send, recv, where):
        return pltpu.make_async_remote_copy(
            src_ref=src, dst_ref=dst, send_sem=send, recv_sem=recv,
            device_id=where, device_id_type=MESH,
        )

    rim_copy = remote(tails, rims, s_rim, r_rim, {"seq": lax.rem(s + 1, ns)})

    @pl.when(s < ns - 1)
    def _():
        rim_copy.start()

    rate[...] = jnp.exp(a_log[...]) * (-LOG2E)
    where_rows = s * rows - PAD + lax.broadcasted_iota(jnp.int32, (rows + PAD, pos.shape[1]), 0)
    hits = jnp.max((where_rows == pos[...]).astype(jnp.float32), axis=1, keepdims=True)
    chosen = mode[...]
    take_signal = hits * (chosen != 1).astype(jnp.float32) > 0.5
    take_gate = (hits * (chosen != 0).astype(jnp.float32) > 0.5)[PAD:]

    @pl.when(s == 0)
    def _():
        rims[...] = jnp.zeros_like(rims)

    @pl.when(s > 0)
    def _():
        rim_copy.wait_recv()

    lb = lanes(inner, 256)

    def conv(i, _):
        col = pl.ds(pl.multiple_of(i * lb, lb), lb)
        edge = rims[:, col].astype(jnp.float32)
        ext[0, 0:PAD, :] = edge
        ext[1, 0:PAD, :] = pltpu.roll(edge, 4, 0)
        ext[0, PAD:, :] = clean[:, col].astype(jnp.float32)
        ext[1, PAD:, :] = corrupt[:, col].astype(jnp.float32)
        ext[2] = jnp.where(take_signal, ext[0], ext[1])
        for r in range(3):
            total = cb[:, col] + cw[0:1, col] * ext[r, PAD - taps + 1 : PAD - taps + 1 + rows, :]
            for k in range(1, taps):
                first = PAD - taps + 1 + k
                total = total + cw[k : k + 1, col] * ext[r, first : first + rows, :]
            rounded = (total / (1.0 + jnp.exp(-total))).astype(jnp.bfloat16)
            act16[r * rows : (r + 1) * rows, col] = rounded
            act[r, :, col] = rounded.astype(jnp.float32)
        return 0

    lax.fori_loop(0, inner // lb, conv, 0)
    width = xw.shape[0]
    proj[...] = jnp.zeros_like(proj)
    proj[:, :width] = lax.dot_general(
        act16[...], xw[...], (((1,), (1,)), ((), ())), preferred_element_type=jnp.float32
    )
    flipped = proj[:, 128:].T
    first = RANK - 128
    for t in range(3 * rows):
        bsp[t] = jnp.broadcast_to(flipped[first : first + STATE, t : t + 1], (STATE, 128))
        csp[t] = jnp.broadcast_to(flipped[first + STATE : first + 2 * STATE, t : t + 1], (STATE, 128))

    chunks = [(0, v * span), (1, v * span)] + [(2, j * span) for j in range(nv)]
    tb = lanes(span, 256)

    partner = {"seq": lax.rem(s + 1, ns)}
    tot_copies = [remote(tot.at[c], tot_in.at[c], s_tot.at[c], r_tot.at[c], partner) for c in range(len(chunks))]
    even_copies = [remote(ends.at[c], even_end.at[c], s_even.at[c], r_even.at[c], partner) for c in range(len(chunks))]

    onward = [
        remote(carry_out.at[c], carry.at[c], s_car.at[c], r_car.at[c], {"seq": lax.rem(s + 2, ns)})
        for c in range(len(chunks))
    ]
    beside = [
        remote(carry.at[c], carry.at[c], s_back.at[c], r_car.at[c], {"seq": lax.rem(s + ns - 1, ns)})
        for c in range(len(chunks))
    ]

    def enter(c, r, off):
        @pl.when(s < 2)
        def _():
            carry[c] = jnp.zeros((STATE, span), jnp.float32)

        @pl.when(s >= 2)
        def _():
            onward[c].wait_recv()

        @pl.when(odd)
        def _():
            @pl.when(s >= 2)
            def _():
                beside[c].start()

            tot_copies[c].wait_recv()
            even_copies[c].wait_recv()

            def link(i, _):
                here = pl.ds(pl.multiple_of(i * tb, tb), tb)
                col = pl.ds(pl.multiple_of(off + i * tb, tb), tb)
                rates = rate[:, col]
                mine = jnp.exp2(rates * tot_in[c, :, here]) * carry[c, :, here] + even_end[c, :, here]
                carry_out[c, :, here] = jnp.exp2(rates * tot[c, :, here]) * mine + ends[c, :, here]
                inflow[c, :, here] = mine
                return 0

            lax.fori_loop(0, span // tb, link, 0)

            @pl.when(s < ns - 1)
            def _():
                onward[c].start()

        @pl.when(even)
        def _():
            inflow[c] = carry[c]

    early = ((0, 2, 2), (2, 4, 4))

    def enter_late(c):
        begin = max([0] + [high for _, high, lag in early if c < len(chunks) - lag])

        @pl.when(s >= begin)
        def _():
            enter(c, *chunks[c])

    for c, (r, off) in enumerate(chunks):
        low = proj[r * rows : (r + 1) * rows, :RANK].astype(jnp.bfloat16)

        def steps_of(i, _, c=c, off=off, low=low):
            here = pl.ds(pl.multiple_of(i * tb, tb), tb)
            col = pl.ds(pl.multiple_of(off + i * tb, tb), tb)
            raw = jnp.dot(low, dtw[:, col], preferred_element_type=jnp.float32) + dtb[:, col]
            step = jnp.maximum(raw, 0.0) + jnp.log1p(jnp.exp(-jnp.abs(raw)))
            stp[c, :, here] = step
            tot[c, :, here] = jnp.sum(step, axis=0, keepdims=True)
            return 0

        lax.fori_loop(0, span // tb, steps_of, 0)

        @pl.when(even)
        def _(c=c):
            tot_copies[c].start()

        def scan_of(i, _, c=c, r=r, off=off):
            here = pl.ds(pl.multiple_of(i * tb, tb), tb)
            col = pl.ds(pl.multiple_of(off + i * tb, tb), tb)
            rates = rate[:, col]

            def eight(b, carried):
                state, running = carried
                at = pl.ds(pl.multiple_of(b * 8, 8), 8)
                steps = stp[c, at, here]
                flows = steps * act[r, at, col]
                outs, sums = [], []
                for k in range(8):
                    step = steps[k : k + 1]
                    t = r * rows + b * 8 + k
                    state = jnp.exp2(rates * step) * state + flows[k : k + 1] * wide(bsp[t], tb)
                    running = running + step
                    outs.append(jnp.sum(wide(csp[t], tb) * state, axis=0, keepdims=True))
                    sums.append(running)
                acc[c, at, here] = jnp.concatenate(outs, axis=0)
                run[c, at, here] = jnp.concatenate(sums, axis=0)
                return state, running

            zero = (jnp.zeros((STATE, tb), jnp.float32), jnp.zeros((1, tb), jnp.float32))
            state, _ = lax.fori_loop(0, rows // 8, eight, zero)
            ends[c, :, here] = state
            return 0

        lax.fori_loop(0, span // tb, scan_of, 0)

        @pl.when(even)
        def _(c=c):
            even_copies[c].start()

        for low_s, high_s, lag in early:
            if c >= lag:

                @pl.when((s >= low_s) & (s < high_s))
                def _(c=c - lag):
                    enter(c, *chunks[c])

    cor_copies = [
        remote(cut.at[1], whole.at[v], s_cor.at[d - 1], r_cor.at[d - 1], {"var": lax.rem(v + d, nv)})
        for d in range(1, nv)
    ]

    def sq_copy(d):
        return remote(own_sq, sq_in.at[d - 1], s_sq.at[d - 1], r_sq.at[d - 1], {"seq": lax.rem(s + d, ns)})

    def pk_copy(d, j):
        return remote(
            own_pk.at[j], pk_in.at[d - 1, j], s_pk.at[d - 1, j], r_pk.at[d - 1, j], {"seq": lax.rem(s + d, ns)}
        )

    def each(act_on):
        def go(d, _):
            act_on(d)
            return 0

        lax.fori_loop(1, ns, go, 0)

    def finish(c, r, off):
        def piece(i, _):
            here = pl.ds(pl.multiple_of(i * tb, tb), tb)
            col = pl.ds(pl.multiple_of(off + i * tb, tb), tb)
            gcol = pl.ds(pl.multiple_of(inner + off + i * tb, tb), tb)
            rates = rate[:, col]
            entering = inflow[c, :, here]

            def eight(b, _):
                at = pl.ds(pl.multiple_of(b * 8, 8), 8)
                running = run[c, at, here]
                outs = []
                for k in range(8):
                    t = r * rows + b * 8 + k
                    outs.append(
                        jnp.sum(
                            jnp.exp2(rates * running[k : k + 1]) * (wide(csp[t], tb) * entering),
                            axis=0,
                            keepdims=True,
                        )
                    )
                acc[c, at, here] = acc[c, at, here] + jnp.concatenate(outs, axis=0)
                return 0

            lax.fori_loop(0, rows // 8, eight, 0)
            if r == 0:
                gate = clean[:, gcol].astype(jnp.float32)
            elif r == 1:
                gate = corrupt[:, gcol].astype(jnp.float32)
            else:
                gate = jnp.where(
                    take_gate, clean[:, gcol].astype(jnp.float32), corrupt[:, gcol].astype(jnp.float32)
                )
            silu = gate / (1.0 + jnp.exp(-gate))
            result = ((acc[c, :, here] + dsk[:, col] * act[r, :, col]) * silu).astype(jnp.bfloat16)
            if r < 2:
                cut[r, :, here] = result
            else:
                out[:, col] = result
            return 0

        lax.fori_loop(0, span // tb, piece, 0)

    for c in range(2):
        enter_late(c)
        finish(c, *chunks[c])
    for copy in cor_copies:
        copy.start()
    whole[v] = cut[1]
    gap = cut[0].astype(jnp.float32) - cut[1].astype(jnp.float32)
    own_sq[...] = jnp.sum(gap * gap, axis=0, keepdims=True)
    each(lambda d: sq_copy(d).start())
    nrm_copies = [
        remote(nrm, nrm_all.at[v], s_nrm.at[d - 1], r_nrm.at[d - 1], {"var": lax.rem(v + d, nv)})
        for d in range(1, nv)
    ]
    for j in range(nv):
        c = 2 + j
        enter_late(c)
        finish(c, *chunks[c])
        if j == 0:
            for copy in cor_copies:
                copy.wait()
        if j == nv - 1:
            each(lambda d: sq_copy(d).wait())
            nrm[...] = own_sq[...] + jnp.sum(sq_in[...], axis=0)
            for copy in nrm_copies:
                copy.start()
            nrm_all[v] = nrm[...]
        mine = out[:, j * span : (j + 1) * span].astype(jnp.float32)
        own_pk[j] = jnp.max(jnp.abs(mine - whole[j].astype(jnp.float32)), axis=0, keepdims=True)
        each(lambda d, j=j: pk_copy(d, j).start())
    for copy in nrm_copies:
        copy.wait()
    for j in range(nv):
        each(lambda d, j=j: pk_copy(d, j).wait())
        best = jnp.maximum(own_pk[j], jnp.max(pk_in[:, j], axis=0))
        eff[:, j * span : (j + 1) * span] = best / jnp.sqrt(nrm_all[j] / (rows * ns) + TINY)

    @pl.when(s < ns - 1)
    def _():
        rim_copy.wait_send()

    @pl.when(even)
    def _():
        for c in range(len(chunks)):
            tot_copies[c].wait_send()
            even_copies[c].wait_send()

    @pl.when(odd & (s >= 2))
    def _():
        for copy in beside:
            copy.wait_send()

    @pl.when(odd & (s < ns - 1))
    def _():
        for copy in onward:
            copy.wait_send()


def shards(clean, corrupt, pos, mode, a_log, dtb, cw, cb, xw, dtw, dsk):
    ns, nv = lax.axis_size("seq"), lax.axis_size("var")
    rows = clean.shape[0]
    inner = cw.shape[1]
    span = inner // nv
    n = 2 + nv
    f32, b16 = jnp.float32, jnp.bfloat16
    vm = pltpu.VMEM
    dma = pltpu.SemaphoreType.DMA
    lb = lanes(inner, 256)
    out, eff = pl.pallas_call(
        functools.partial(body, ns, nv),
        out_shape=(
            jax.ShapeDtypeStruct((rows, inner), b16),
            jax.ShapeDtypeStruct((1, inner), f32),
        ),
        in_specs=[pl.BlockSpec(memory_space=vm)] * 11,
        out_specs=[pl.BlockSpec(memory_space=vm)] * 2,
        scratch_shapes=[
            vm((8, inner), b16), vm((8, inner), b16),
            vm((3, rows + PAD, lb), f32),
            vm((3 * rows, inner), b16), vm((3, rows, inner), f32),
            vm((3 * rows, 256), f32),
            vm((3 * rows, STATE, 128), f32), vm((3 * rows, STATE, 128), f32),
            vm((STATE, inner), f32),
            vm((n, rows, span), f32), vm((n, rows, span), f32), vm((n, rows, span), f32),
            vm((n, 1, span), f32), vm((n, 1, span), f32),
            vm((n, STATE, span), f32), vm((n, STATE, span), f32),
            vm((n, STATE, span), f32), vm((n, STATE, span), f32), vm((n, STATE, span), f32),
            vm((2, rows, span), b16), vm((nv, rows, span), b16),
            vm((1, span), f32), vm((ns - 1, 1, span), f32),
            vm((nv, 1, span), f32), vm((ns - 1, nv, 1, span), f32),
            vm((1, span), f32), vm((nv, 1, span), f32),
            dma, dma, dma((n,)), dma((n,)),
            dma((n,)), dma((n,)), dma((n,)), dma((n,)), dma((n,)),
            dma((nv - 1,)), dma((nv - 1,)),
            dma((ns - 1,)), dma((ns - 1,)), dma((ns - 1, nv)), dma((ns - 1, nv)),
            dma((nv - 1,)), dma((nv - 1,)),
        ],
        compiler_params=pltpu.CompilerParams(
            collective_id=0, has_side_effects=True, vmem_limit_bytes=60 * 1024 * 1024
        ),
    )(
        clean, corrupt, pos, mode.reshape(1, 1), a_log, dtb.reshape(1, -1), cw,
        cb.reshape(1, -1), xw.T, dtw, dsk.reshape(1, -1),
    )
    return (out[None], eff)


def solution(mesh):
    return jax.shard_map(
        shards,
        mesh=mesh,
        in_specs=(
            P("seq", None), P("seq", None), P("var", None), P("var"),
            P(), P(), P(), P(), P(), P(), P(),
        ),
        out_specs=(P("var", "seq", None), P("var", None)),
        check_vma=False,
    )
```
